32 devices in a mesh: dp: 16 (over z, x, core), rep: 2 (over y).
Axes of the slice: x: 2, y: 2, z: 4, core: 2. Of those that a mesh axis runs over, the one named last changes fastest.
Arguments:
- images: bfloat16 [16384, 512], P(('dp', 'rep')), may hold values from -6 to 6
- text_feats: bfloat16 [16384, 768], P(('dp', 'rep')), may hold values from -6 to 6
- text_proj: bfloat16 [768, 512], replicated, may hold values from -0.21875 to 0.21875
- logit_scale: float32 [1], replicated, may hold values from 4 to 16
- logit_bias: float32 [1], replicated, may hold values from -6 to -2
Outputs:
- image_grad: bfloat16 [16384, 512], P(('dp', 'rep'))
- proj_grad: float32 [768, 512], P(('dp', 'rep'))
The draws below stay inside these ranges and needn't reach their ends.
All inputs are finite; a program needn't handle non-finite values.
Results may differ from the reference program's by a relative error of at most 0.013.
Values may be sent and summed in bfloat16 or wider, within the bound.
A program may use at most 64 MiB of HBM per device.

```python
import math
import jax
import jax.numpy as jnp
from jax import lax

E = 512
D_TEXT = 768
ROWS = 512
SHIFTS = 8
BATCH = 16384
N_DP = 16
N_REP = 2


def strengthened(values, rng, source, target, blocks, factor):
    owner, partner = [(jnp.arange(values.shape[position]) // (values.shape[position] // blocks)).reshape([-1 if axis == position else 1 for axis in range(values.ndim)]) for position in (source, target)]
    chosen = jax.random.permutation(rng, blocks)[partner]
    strong = (owner == chosen) | (owner == (partner + blocks // 2) % blocks)
    return jnp.where(strong, factor * values, values)


def level_of(own_key, shape, shards, low, high):
    level = 1.0
    for dim, blocks in shards:
        draws = jax.random.uniform(jax.random.fold_in(jax.random.fold_in(own_key, 6), dim), (blocks,), jnp.float32, low / len(shards), high / len(shards))
        level = level * jnp.repeat(jnp.exp(draws), shape[dim] // blocks).reshape((-1,) + (1,) * (len(shape) - 1 - dim))
    return level


def gaussian(stream_key, shape, scale, limit, cuts=(), kind=jnp.bfloat16):
    values = scale * jax.random.normal(stream_key, shape, jnp.float32)
    if cuts:
        values = values * level_of(stream_key, shape, cuts, -0.22, 0.18)
    return jnp.clip(values, -limit, limit).astype(kind)


def bell_draw_with(rng, dims, width, bound, shards, heavy, kind=jnp.bfloat16):
    values = width * jax.random.normal(rng, dims, jnp.float32)
    if shards:
        values = values * level_of(rng, dims, shards, -0.22, 0.18)
    return jnp.clip(strengthened(values, jax.random.fold_in(rng, 3), *heavy), -bound, bound).astype(kind)


def setup_inputs(seed: int = 0) -> dict:
    keys = jax.random.split(jax.random.key(seed), 6)
    images = gaussian(keys[0], (BATCH, E), 1.0, 6.0, ((0, 32),))
    text_feats = bell_draw_with(keys[1], (BATCH, D_TEXT), 1.0, 6.0, ((0, 32),), (0, 1, 32, 2.75))
    text_proj = gaussian(keys[2], (D_TEXT, E), D_TEXT ** -0.5, 0.21875)
    logit_scale = jnp.clip(jnp.exp(jax.random.uniform(keys[3], (1,), jnp.float32, math.log(4.0), math.log(16.0))), 4.0, 16.0)
    logit_bias = jnp.clip(jax.random.uniform(keys[4], (1,), jnp.float32, -6.0, -2.0), -6.0, -2.0)
    return {"images": images, "text_feats": text_feats, "text_proj": text_proj, "logit_scale": logit_scale, "logit_bias": logit_bias}


EPS = 1e-06

def unit_rows(values):
    square = lax.optimization_barrier(jnp.sum(values * values, axis=-1, keepdims=True))
    factor = lax.rsqrt(square + EPS)
    return (values * factor, factor)

def back_rows(normal, factor, upstream):
    return factor * (upstream - normal * lax.optimization_barrier(jnp.sum(normal * upstream, axis=-1, keepdims=True)))

def reference(images, text_feats, text_proj, logit_scale, logit_bias):
    blocks = N_DP * N_REP
    image_unit, image_factor = unit_rows(images.astype(jnp.float32))
    u_round = lax.optimization_barrier(image_unit.astype(jnp.bfloat16))
    text_raw = jnp.dot(text_feats, text_proj, preferred_element_type=jnp.float32)
    text_unit, text_factor = unit_rows(text_raw)
    v_round = lax.optimization_barrier(text_unit.astype(jnp.bfloat16))
    u_blocks = u_round.astype(jnp.float32).reshape(blocks, ROWS, E)
    v_blocks = v_round.astype(jnp.float32).reshape(blocks, ROWS, E)
    scaling = logit_scale[0]
    shifted = logit_bias[0]
    positions = jnp.arange(ROWS, dtype=jnp.int32)
    identity_mask = (positions[:, None] == positions[None, :]).astype(jnp.float32)
    image_sum = jnp.zeros((blocks, ROWS, E), jnp.float32)
    text_sum = jnp.zeros((blocks, ROWS, E), jnp.float32)
    for offset in range(SHIFTS + 1):
        held = jnp.roll(v_blocks, offset * N_REP, axis=0)
        logits = scaling * jnp.einsum('brd,bcd->brc', u_blocks, held) + shifted
        if offset == 0:
            label = 2.0 * identity_mask - 1.0
        else:
            label = -jnp.ones((ROWS, ROWS), jnp.float32)
        weighted = scaling * -label * jax.nn.sigmoid(-label * logits)
        weighted = lax.optimization_barrier(weighted.astype(jnp.bfloat16)).astype(jnp.float32)
        image_sum = image_sum + jnp.einsum('brc,bcd->brd', weighted, held)
        returned = jnp.einsum('brc,brd->bcd', weighted, u_blocks)
        text_sum = text_sum + jnp.roll(returned, -offset * N_REP, axis=0)
    image_grad = back_rows(image_unit, image_factor, image_sum.reshape(-1, E)).astype(jnp.bfloat16)
    text_grad = back_rows(text_unit, text_factor, text_sum.reshape(-1, E)).astype(jnp.bfloat16)
    proj_grad = lax.dot_general(text_feats, text_grad, (((0,), (0,)), ((), ())), preferred_element_type=jnp.float32)
    return (image_grad, proj_grad)
```

```python
import functools

import jax
import jax.numpy as jnp
from jax import lax
from jax.experimental import pallas as pl
from jax.experimental.pallas import tpu as pltpu
from jax.sharding import PartitionSpec as P

MESH = pl.DeviceIdType.MESH
EPS = 1e-06
SHIFTS = 8
SPAN = 4
CHUNKS = 4
LAG = 3
LEAD = 2
LOG2E = 1.4426950408889634


def kernel(
    n_dp, n_rep, summed,
    scale_ref, bias_ref, images_hbm, feats_hbm, proj_hbm, image_hbm, proj_out_hbm,
    blocks, sums, raw, factors, partial, images_ref, feats_ref, proj_ref, image_out, proj_out,
    load, store, send_z, send_x, send_c, recv,
    pieces, out1, in1, out2, in2, out3, in3, out4, in4, rs_send, rs_recv,
):
    rows = images_hbm.shape[0]
    piece = rows // CHUNKS
    half = min(256, rows)
    dp = lax.axis_index("dp")
    rep = lax.axis_index("rep")
    n_z = n_dp // SPAN
    q = lax.rem(dp, SPAN)
    z = dp // SPAN
    x = q // 2
    c = lax.rem(q, 2)
    to_x = dp + 2 - 4 * x
    to_c = dp + 1 - 2 * c
    q_x = q + 2 - 4 * x
    q_c = q + 1 - 2 * c
    q_xc = q_x + 1 - 2 * c
    up = lax.rem(dp + SPAN, n_dp)
    down = lax.rem(dp + n_dp - SPAN, n_dp)

    barrier = pltpu.get_barrier_semaphore()
    greeted = 2
    for target in (to_x, to_c):
        pl.semaphore_signal(barrier, inc=1, device_id={"dp": target}, device_id_type=MESH)
    if summed:
        for step in range(1, n_z):
            pl.semaphore_signal(
                barrier, inc=1, device_id={"dp": lax.rem(dp + SPAN * step, n_dp)}, device_id_type=MESH
            )
        pl.semaphore_signal(barrier, inc=1, device_id={"rep": 1 - rep}, device_id_type=MESH)
        greeted += n_z
    else:
        for target in (up, down):
            pl.semaphore_signal(barrier, inc=1, device_id={"dp": target}, device_id_type=MESH)
        greeted += 2

    loads = [
        pltpu.make_async_copy(source, target, load.at[n])
        for n, (source, target) in enumerate(
            ((images_hbm, images_ref), (proj_hbm, proj_ref), (feats_hbm, feats_ref))
        )
    ]
    for copy in loads:
        copy.start()

    def slot_of(kind, r, place):
        return (kind * 3 + r) * SPAN + place

    def moved(source, target, h, send, dev):
        return pltpu.make_async_remote_copy(
            src_ref=blocks.at[source, pl.ds(h * piece, piece), :],
            dst_ref=blocks.at[target, pl.ds(h * piece, piece), :],
            send_sem=send,
            recv_sem=recv.at[target * CHUNKS + h],
            device_id={"dp": dev},
            device_id_type=MESH,
        )

    def z_copy(kind, r, h):
        dev = jnp.where(kind == 0, down, up)
        return moved(
            slot_of(kind, r, q), slot_of(kind, r + 1, q), h, send_z.at[(kind * 2 + r) * CHUNKS + h], dev
        )

    def first_of(kind, bit):
        return jnp.where(kind == 0, 1 - bit, bit)

    def x_copy(kind, r, h):
        s = slot_of(kind, r, q)
        e = kind * 2 + r - first_of(kind, x)
        return moved(s, s, h, send_x.at[e * CHUNKS + h], to_x)

    def c_copy(kind, r, h):
        s = slot_of(kind, r, q)
        e = kind * 2 + r - first_of(kind, c)
        return moved(s, s, h, send_c.at[e * CHUNKS + h], to_c)

    def relay_copy(kind, e, h):
        s = slot_of(kind, first_of(kind, 1 - x) + e, q_x)
        return moved(s, s, h, send_c.at[(4 + kind * 2 + e) * CHUNKS + h], to_c)

    def arrived(s, h):
        view = blocks.at[s, pl.ds(h * piece, piece), :]
        pltpu.make_async_copy(view, view, recv.at[s * CHUNKS + h]).wait()

    def start_own(kind, along=True, across=True):
        first = first_of(kind, x)
        first_c = first_of(kind, c)
        @pl.loop(0, CHUNKS)
        def _(h):
            if along:
                z_copy(kind, 0, h).start()

            @pl.when((first == 0) & across)
            def _():
                x_copy(kind, 0, h).start()

            @pl.when((first_c == 0) & across)
            def _():
                c_copy(kind, 0, h).start()

    scaling = scale_ref[0]
    shifted = bias_ref[0]
    own_u = slot_of(0, 0, q)
    own_v = slot_of(1, 0, q)

    loads[0].wait()

    @pl.loop(0, rows // half)
    def _(i):
        part = pl.ds(i * half, half)
        values = images_ref[part, :].astype(jnp.float32)
        factor = lax.rsqrt(jnp.sum(values * values, axis=-1, keepdims=True) + EPS)
        factors[0, part, :] = factor
        blocks[own_u, part, :] = (values * factor).astype(jnp.bfloat16)

    loads[1].wait()
    loads[2].wait()

    @pl.loop(0, rows // half)
    def _(i):
        part = pl.ds(i * half, half)
        values = jnp.dot(feats_ref[part, :], proj_ref[...], preferred_element_type=jnp.float32)
        factor = lax.rsqrt(jnp.sum(values * values, axis=-1, keepdims=True) + EPS)
        raw[part, :] = values
        factors[1, part, :] = factor
        blocks[own_v, part, :] = (values * factor).astype(jnp.bfloat16)

    pl.semaphore_wait(barrier, greeted)
    start_own(0)
    start_own(1, False, True)

    slope = scaling * -LOG2E
    offset = shifted * -LOG2E

    def score(own, part, s, cut):
        return lax.dot_general(
            blocks[own, part, :], blocks[s, cut, :], (((1,), (1,)), ((), ())),
            preferred_element_type=jnp.float32,
        )

    def own_tile(kind):
        own = slot_of(1 - kind, 0, q)
        s = slot_of(kind, 0, q)
        for i in range(rows // half):
            part = pl.ds(i * half, half)
            logits = scaling * score(own, part, s, pl.ds(0, rows)) + shifted
            line = lax.broadcasted_iota(jnp.int32, logits.shape, 0) + i * half
            paired = line == lax.broadcasted_iota(jnp.int32, logits.shape, 1)
            weight = jnp.where(paired, -scaling, scaling) * jax.nn.sigmoid(
                jnp.where(paired, -logits, logits)
            )
            sums[kind, part, :] = jnp.dot(
                weight.astype(jnp.bfloat16), blocks[s], preferred_element_type=jnp.float32
            )

    def tile(kind, cuts):
        own = slot_of(1 - kind, 0, q)
        strips = [pl.ds(i * half, half) for i in range(rows // half)]
        weights = []
        for part in strips:
            for s, cut in cuts:
                grown = 1.0 + jnp.exp2(slope * score(own, part, s, cut) + offset)
                weight = scaling * pltpu.reciprocal(grown, approx=True)
                weights.append(weight.astype(jnp.bfloat16))
        for i, part in enumerate(strips):
            total = sums[kind, part, :]
            for j, (s, cut) in enumerate(cuts):
                total += jnp.dot(
                    weights[i * len(cuts) + j], blocks[s, cut, :],
                    preferred_element_type=jnp.float32,
                )
            sums[kind, part, :] = total

    def x_step(t):
        phase = t // CHUNKS
        h = lax.rem(t, CHUNKS)
        kind = phase // 2
        e = lax.rem(phase, 2)
        arrived(slot_of(kind, first_of(kind, 1 - x) + e, q_x), h)
        relay_copy(kind, e, h).start()

    def block_of(t):
        phase = t // 4
        i = lax.rem(t, 4)
        kind = phase // 2
        e = lax.rem(phase, 2)
        bit = jnp.where(i == 1, 1 - c, 1 - x)
        r = e + jnp.where(i == 0, 1, first_of(kind, bit))
        place = jnp.where(i == 0, q, jnp.where(i == 1, q_c, jnp.where(i == 2, q_x, q_xc)))
        return kind, slot_of(kind, r, place), i

    def tile_step(t):
        kind, s, i = block_of(t)

        @pl.when(lax.rem(i, 2) == 1)
        def _():
            @pl.loop(0, CHUNKS)
            def _(h):
                arrived(s, h)

        tile(kind, [(s, pl.ds(0, rows))])

    def pair_part(t, part):
        near = CHUNKS // 2
        cut = pl.ds(pl.multiple_of(part * (rows // 2), 16), rows // 2)
        kind, s, _ = block_of(t)
        _, other, _ = block_of(t + 1)

        @pl.loop(0, near)
        def _(h):
            arrived(other, part * near + h)

        tile(kind, [(s, cut), (other, cut)])

    def exchange(stage, source, target, dev):
        return pltpu.make_async_remote_copy(
            src_ref=source, dst_ref=target, send_sem=rs_send.at[stage], recv_sem=rs_recv.at[stage],
            device_id=dev, device_id_type=MESH,
        )

    def text_back(i):
        part = pl.ds(i * half, half)
        factor = factors[1, part, :]
        normal = raw[part, :] * factor
        upstream = sums[0, part, :]
        return factor * (upstream - normal * jnp.sum(normal * upstream, axis=-1, keepdims=True))

    def proj_partial():
        @pl.loop(0, rows // half)
        def _(i):
            raw[pl.ds(i * half, half), :] = text_back(i)

        text_grad = raw[...].astype(jnp.bfloat16)
        wide = 256

        @pl.loop(0, feats_ref.shape[1] // wide)
        def _(i):
            cols = pl.ds(pl.multiple_of(i * wide, wide), wide)
            partial[pl.ds(pl.multiple_of(i * wide, wide), wide), :] = lax.dot_general(
                feats_ref[:, cols], text_grad, (((0,), (0,)), ((), ())),
                preferred_element_type=jnp.float32,
            )

    if summed:
        quarter = n_z
        tall = proj_out.shape[0]
        deep = proj_out.shape[1] // 2

        def fill(ref, base):
            @pl.loop(0, ref.shape[0])
            def _(j):
                ref[j] = pieces[base + j].astype(jnp.bfloat16)

        def gain(ref, base):
            @pl.loop(0, ref.shape[0])
            def _(j):
                pieces[base + j] += ref[j].astype(jnp.float32)

        base1 = c * 4 * quarter
        base2 = base1 + rep * 2 * quarter
        base3 = base2 + x * quarter
        stage_c = exchange(0, out1, in1, {"dp": to_c})
        stage_y = exchange(1, out2, in2, {"rep": 1 - rep})
        stage_x = exchange(2, out3, in3, {"dp": to_x})

        def stage_z(step):
            row = lax.rem(z + step, n_z)
            return exchange(
                2 + step, out4.at[row], in4.at[step - 1], {"dp": lax.rem(dp + SPAN * step, n_dp)}
            )

        def rs0():
            @pl.loop(0, 8 * n_z)
            def _(i):
                place = (lax.rem(i, 4) * 2 + lax.rem(i // 4, 2)) * n_z + i // 8
                lines = partial[pl.ds(pl.multiple_of(i * tall, 8), tall), :]
                pieces[place, pl.ds(0, tall), :] = lines[:, :deep]
                pieces[place, pl.ds(tall, tall), :] = lines[:, deep:]

            fill(out1, (1 - c) * 4 * quarter)
            stage_c.start()

        def rs1():
            stage_c.wait()
            gain(in1, base1)
            fill(out2, base1 + (1 - rep) * 2 * quarter)
            stage_y.start()

        def rs2():
            stage_y.wait()
            gain(in2, base2)
            fill(out3, base2 + (1 - x) * quarter)
            stage_x.start()

        def rs3():
            stage_x.wait()
            gain(in3, base3)
            fill(out4, base3)
            for step in range(1, n_z):
                stage_z(step).start()

        def rs4():
            total = pieces[base3 + z]
            for step in range(1, n_z):
                stage_z(step).wait()
                total = total + in4[step - 1].astype(jnp.float32)
            proj_out[:, :deep] = total[:tall]
            proj_out[:, deep:] = total[tall:]

    @pl.loop(0, 4 * CHUNKS)
    def _(s):
        phase = s // CHUNKS
        h = lax.rem(s, CHUNKS)
        kind = phase // 2
        r = 1 + lax.rem(phase, 2)
        arrived(slot_of(kind, r, q), h)

        @pl.when(r == 1)
        def _():
            z_copy(kind, 1, h).start()

        @pl.when(r <= first_of(kind, x) + 1)
        def _():
            x_copy(kind, r, h).start()

        @pl.when(r <= first_of(kind, c) + 1)
        def _():
            c_copy(kind, r, h).start()

        @pl.when(s == 2 * CHUNKS - LEAD)
        def _():
            start_own(1, True, False)

        @pl.when(s >= LAG)
        def _():
            x_step(s - LAG)

        @pl.when(s < 2)
        def _():
            own_tile(s)

        if CHUNKS == 4:
            @pl.when(s >= CHUNKS)
            def _():
                tile_step(s - CHUNKS)

        if summed:
            for at, stage in enumerate((proj_partial, rs0, rs1, rs2, rs3)):
                @pl.when(s == 3 * CHUNKS - 1 + at)
                def _():
                    stage()

    last = 4 * CHUNKS - LAG

    @pl.loop(0, 4)
    def _(n):
        @pl.when(n < 3)
        def _():
            x_step(last + n)

        pair_part(12 + 2 * lax.rem(n, 2), n // 2)

    if summed:
        rs4()

    if not summed:
        proj_partial()
        proj_out[...] = partial[...]
    proj_store = pltpu.make_async_copy(proj_out, proj_out_hbm, store.at[0])
    proj_store.start()

    @pl.loop(0, rows // half)
    def _(i):
        part = pl.ds(i * half, half)
        factor = factors[0, part, :]
        normal = images_ref[part, :].astype(jnp.float32) * factor
        upstream = sums[1, part, :]
        image_out[part, :] = (
            factor * (upstream - normal * jnp.sum(normal * upstream, axis=-1, keepdims=True))
        ).astype(jnp.bfloat16)

    image_store = pltpu.make_async_copy(image_out, image_hbm, store.at[1])
    image_store.start()

    @pl.loop(0, 4 * CHUNKS)
    def _(t):
        h = lax.rem(t, CHUNKS)
        i = t // CHUNKS
        kind = i // 2
        e = lax.rem(i, 2)
        z_copy(kind, e, h).wait_send()
        x_copy(kind, first_of(kind, x) + e, h).wait_send()
        c_copy(kind, first_of(kind, c) + e, h).wait_send()
        relay_copy(kind, e, h).wait_send()

    image_store.wait()
    proj_store.wait()


def solution(mesh):
    n_dp, n_rep = mesh.shape["dp"], mesh.shape["rep"]

    def on_device(images, feats, proj, scale, bias):
        rows, width = images.shape
        depth = feats.shape[1]
        share = depth // (n_dp * n_rep)
        n_z = n_dp // SPAN
        summed = n_rep == 2 and share % 8 == 0
        lines = share if summed else depth
        unit = (2 * lines, width // 2) if summed else (16, 128)
        near = n_z if summed else 1
        hbm = pl.BlockSpec(memory_space=pltpu.HBM)
        anywhere = pl.BlockSpec(memory_space=pl.ANY)
        smem = pl.BlockSpec(memory_space=pltpu.SMEM)
        dma = pltpu.SemaphoreType.DMA
        image_grad, proj_grad = pl.pallas_call(
            functools.partial(kernel, n_dp, n_rep, summed),
            out_shape=(
                jax.ShapeDtypeStruct((rows, width), jnp.bfloat16),
                jax.ShapeDtypeStruct((lines, width), jnp.float32),
            ),
            in_specs=[smem, smem, hbm, hbm, hbm],
            out_specs=(anywhere, anywhere),
            scratch_shapes=[
                pltpu.VMEM((6 * SPAN, rows, width), jnp.bfloat16),
                pltpu.VMEM((2, rows, width), jnp.float32),
                pltpu.VMEM((rows, width), jnp.float32),
                pltpu.VMEM((2, rows, 1), jnp.float32),
                pltpu.VMEM((depth, width), jnp.float32),
                pltpu.VMEM((rows, width), jnp.bfloat16),
                pltpu.VMEM((rows, depth), jnp.bfloat16),
                pltpu.VMEM((depth, width), jnp.bfloat16),
                pltpu.VMEM((rows, width), jnp.bfloat16),
                pltpu.VMEM((lines, width), jnp.float32),
                dma((3,)),
                dma((2,)),
                dma((4 * CHUNKS,)),
                dma((4 * CHUNKS,)),
                dma((8 * CHUNKS,)),
                dma((6 * SPAN * CHUNKS,)),
                pltpu.VMEM((8 * near,) + unit, jnp.float32),
                pltpu.VMEM((4 * near,) + unit, jnp.bfloat16),
                pltpu.VMEM((4 * near,) + unit, jnp.bfloat16),
                pltpu.VMEM((2 * near,) + unit, jnp.bfloat16),
                pltpu.VMEM((2 * near,) + unit, jnp.bfloat16),
                pltpu.VMEM((near,) + unit, jnp.bfloat16),
                pltpu.VMEM((near,) + unit, jnp.bfloat16),
                pltpu.VMEM((near,) + unit, jnp.bfloat16),
                pltpu.VMEM((near,) + unit, jnp.bfloat16),
                dma((3 + near,)),
                dma((3 + near,)),
            ],
            compiler_params=pltpu.CompilerParams(
                collective_id=0, has_side_effects=True, vmem_limit_bytes=54400 << 10
            ),
        )(scale, bias, images, feats, proj)
        if not summed:
            proj_grad = lax.psum_scatter(
                proj_grad, ("dp", "rep"), scatter_dimension=0, tiled=True
            )
        return image_grad, proj_grad

    in_specs = (P(("dp", "rep"), None), P(("dp", "rep"), None), P(), P(), P())
    out_specs = (P(("dp", "rep"), None), P(("dp", "rep"), None))
    return jax.shard_map(
        on_device, mesh=mesh, in_specs=in_specs, out_specs=out_specs, check_vma=False
    )
```

```python
import functools

import jax
import jax.numpy as jnp
from jax import lax
from jax.experimental import pallas as pl
from jax.experimental.pallas import tpu as pltpu
from jax.sharding import PartitionSpec as P

MESH = pl.DeviceIdType.MESH
EPS = 1e-06
SHIFTS = 8
SPAN = 4
CHUNKS = 4
LAG = 3
LEAD = 3
STAGES = (11, 12, 14, 17)
LOG2E = 1.4426950408889634


def kernel(
    n_dp, n_rep, summed,
    scale_ref, bias_ref, images_hbm, feats_hbm, proj_hbm, image_hbm, proj_out_hbm,
    blocks, sums, raw, factors, partial, images_ref, feats_ref, proj_ref, image_out, proj_out,
    feats_turned, load, store, send_z, send_x, send_c, recv,
    pieces, out1, in1, out2, in2, out3, in3, out4, in4, rs_send, rs_recv,
):
    rows = images_hbm.shape[0]
    piece = rows // CHUNKS
    half = min(256, rows)
    dp = lax.axis_index("dp")
    rep = lax.axis_index("rep")
    n_z = n_dp // SPAN
    q = lax.rem(dp, SPAN)
    z = dp // SPAN
    x = q // 2
    c = lax.rem(q, 2)
    to_x = dp + 2 - 4 * x
    to_c = dp + 1 - 2 * c
    q_x = q + 2 - 4 * x
    q_c = q + 1 - 2 * c
    q_xc = q_x + 1 - 2 * c
    up = lax.rem(dp + SPAN, n_dp)
    down = lax.rem(dp + n_dp - SPAN, n_dp)

    barrier = pltpu.get_barrier_semaphore()
    greeted = 2
    for target in (to_x, to_c):
        pl.semaphore_signal(barrier, inc=1, device_id={"dp": target}, device_id_type=MESH)
    if summed:
        for step in range(1, n_z):
            pl.semaphore_signal(
                barrier, inc=1, device_id={"dp": lax.rem(dp + SPAN * step, n_dp)}, device_id_type=MESH
            )
        pl.semaphore_signal(barrier, inc=1, device_id={"rep": 1 - rep}, device_id_type=MESH)
        greeted += n_z
    else:
        for target in (up, down):
            pl.semaphore_signal(barrier, inc=1, device_id={"dp": target}, device_id_type=MESH)
        greeted += 2

    loads = [
        pltpu.make_async_copy(source, target, load.at[n])
        for n, (source, target) in enumerate(
            ((images_hbm, images_ref), (proj_hbm, proj_ref), (feats_hbm, feats_ref))
        )
    ]
    for copy in loads:
        copy.start()

    def slot_of(kind, r, place):
        return (kind * 3 + r) * SPAN + place

    def moved(source, target, h, send, dev):
        return pltpu.make_async_remote_copy(
            src_ref=blocks.at[source, pl.ds(h * piece, piece), :],
            dst_ref=blocks.at[target, pl.ds(h * piece, piece), :],
            send_sem=send,
            recv_sem=recv.at[target * CHUNKS + h],
            device_id={"dp": dev},
            device_id_type=MESH,
        )

    def z_copy(kind, r, h):
        dev = jnp.where(kind == 0, down, up)
        return moved(
            slot_of(kind, r, q), slot_of(kind, r + 1, q), h, send_z.at[(kind * 2 + r) * CHUNKS + h], dev
        )

    def first_of(kind, bit):
        return jnp.where(kind == 0, 1 - bit, bit)

    def x_copy(kind, r, h):
        s = slot_of(kind, r, q)
        e = kind * 2 + r - first_of(kind, x)
        return moved(s, s, h, send_x.at[e * CHUNKS + h], to_x)

    def c_copy(kind, r, h):
        s = slot_of(kind, r, q)
        e = kind * 2 + r - first_of(kind, c)
        return moved(s, s, h, send_c.at[e * CHUNKS + h], to_c)

    def relay_copy(kind, e, h):
        s = slot_of(kind, first_of(kind, 1 - x) + e, q_x)
        return moved(s, s, h, send_c.at[(4 + kind * 2 + e) * CHUNKS + h], to_c)

    def arrived(s, h):
        view = blocks.at[s, pl.ds(h * piece, piece), :]
        pltpu.make_async_copy(view, view, recv.at[s * CHUNKS + h]).wait()

    def start_own(kind, along=True, across=True):
        first = first_of(kind, x)
        first_c = first_of(kind, c)
        @pl.loop(0, CHUNKS)
        def _(h):
            if along:
                z_copy(kind, 0, h).start()

            @pl.when((first == 0) & across)
            def _():
                x_copy(kind, 0, h).start()

            @pl.when((first_c == 0) & across)
            def _():
                c_copy(kind, 0, h).start()

    scaling = scale_ref[0]
    shifted = bias_ref[0]
    own_u = slot_of(0, 0, q)
    own_v = slot_of(1, 0, q)

    loads[0].wait()

    @pl.loop(0, rows // half)
    def _(i):
        part = pl.ds(i * half, half)
        values = images_ref[part, :].astype(jnp.float32)
        factor = lax.rsqrt(jnp.sum(values * values, axis=-1, keepdims=True) + EPS)
        factors[0, part, :] = factor
        blocks[own_u, part, :] = (values * factor).astype(jnp.bfloat16)

    loads[1].wait()
    loads[2].wait()

    @pl.loop(0, rows // half)
    def _(i):
        part = pl.ds(i * half, half)
        values = jnp.dot(feats_ref[part, :], proj_ref[...], preferred_element_type=jnp.float32)
        factor = lax.rsqrt(jnp.sum(values * values, axis=-1, keepdims=True) + EPS)
        raw[part, :] = values
        factors[1, part, :] = factor
        blocks[own_v, part, :] = (values * factor).astype(jnp.bfloat16)

    if summed:
        feats_turned[...] = feats_ref[...].T

    pl.semaphore_wait(barrier, greeted)
    start_own(0)
    start_own(1, False, True)

    slope = scaling * -LOG2E
    offset = shifted * -LOG2E

    def score(own, part, s, cut):
        return lax.dot_general(
            blocks[own, part, :], blocks[s, cut, :], (((1,), (1,)), ((), ())),
            preferred_element_type=jnp.float32,
        )

    def own_tile(kind):
        own = slot_of(1 - kind, 0, q)
        s = slot_of(kind, 0, q)
        for i in range(rows // half):
            part = pl.ds(i * half, half)
            logits = scaling * score(own, part, s, pl.ds(0, rows)) + shifted
            line = lax.broadcasted_iota(jnp.int32, logits.shape, 0) + i * half
            paired = line == lax.broadcasted_iota(jnp.int32, logits.shape, 1)
            weight = jnp.where(paired, -scaling, scaling) * jax.nn.sigmoid(
                jnp.where(paired, -logits, logits)
            )
            sums[kind, part, :] = jnp.dot(
                weight.astype(jnp.bfloat16), blocks[s], preferred_element_type=jnp.float32
            )

    def tile(kind, cuts):
        own = slot_of(1 - kind, 0, q)
        strips = [pl.ds(i * half, half) for i in range(rows // half)]
        weights = []
        for part in strips:
            for s, cut in cuts:
                grown = 1.0 + jnp.exp2(slope * score(own, part, s, cut) + offset)
                weight = scaling * pltpu.reciprocal(grown, approx=True)
                weights.append(weight.astype(jnp.bfloat16))
        for i, part in enumerate(strips):
            total = sums[kind, part, :]
            for j, (s, cut) in enumerate(cuts):
                total += jnp.dot(
                    weights[i * len(cuts) + j], blocks[s, cut, :],
                    preferred_element_type=jnp.float32,
                )
            sums[kind, part, :] = total

    def x_step(t):
        phase = t // CHUNKS
        h = lax.rem(t, CHUNKS)
        kind = phase // 2
        e = lax.rem(phase, 2)
        arrived(slot_of(kind, first_of(kind, 1 - x) + e, q_x), h)
        relay_copy(kind, e, h).start()

    def block_of(t):
        phase = t // 4
        i = lax.rem(t, 4)
        kind = phase // 2
        e = lax.rem(phase, 2)
        bit = jnp.where(i == 1, 1 - c, 1 - x)
        r = e + jnp.where(i == 0, 1, first_of(kind, bit))
        place = jnp.where(i == 0, q, jnp.where(i == 1, q_c, jnp.where(i == 2, q_x, q_xc)))
        return kind, slot_of(kind, r, place), i

    def tile_step(t):
        kind, s, i = block_of(t)

        @pl.when(lax.rem(i, 2) == 1)
        def _():
            @pl.loop(0, CHUNKS)
            def _(h):
                arrived(s, h)

        tile(kind, [(s, pl.ds(0, rows))])

    def pair_part(t, part):
        near = CHUNKS // 2
        cut = pl.ds(pl.multiple_of(part * (rows // 2), 16), rows // 2)
        kind, s, _ = block_of(t)
        _, other, _ = block_of(t + 1)

        @pl.loop(0, near)
        def _(h):
            arrived(other, part * near + h)

        tile(kind, [(s, cut), (other, cut)])

    def exchange(stage, source, target, dev):
        return pltpu.make_async_remote_copy(
            src_ref=source, dst_ref=target, send_sem=rs_send.at[stage], recv_sem=rs_recv.at[stage],
            device_id=dev, device_id_type=MESH,
        )

    def text_back(i):
        part = pl.ds(i * half, half)
        factor = factors[1, part, :]
        normal = raw[part, :] * factor
        upstream = sums[0, part, :]
        return factor * (upstream - normal * jnp.sum(normal * upstream, axis=-1, keepdims=True))

    def text_grads():
        @pl.loop(0, rows // half)
        def _(i):
            image_out[pl.ds(i * half, half), :] = text_back(i).astype(jnp.bfloat16)

    def proj_partial():
        text_grads()
        text_grad = image_out[...]
        wide = 256

        @pl.loop(0, feats_ref.shape[1] // wide)
        def _(i):
            cols = pl.ds(pl.multiple_of(i * wide, wide), wide)
            partial[pl.ds(pl.multiple_of(i * wide, wide), wide), :] = lax.dot_general(
                feats_ref[:, cols], text_grad, (((0,), (0,)), ((), ())),
                preferred_element_type=jnp.float32,
            )

    if summed:
        quarter = n_z
        tall = proj_out.shape[0]
        deep = proj_out.shape[1] // 2

        def fill(ref, base):
            @pl.loop(0, ref.shape[0])
            def _(j):
                ref[j] = pieces[base + j].astype(jnp.bfloat16)

        def gain(ref, base):
            @pl.loop(0, ref.shape[0])
            def _(j):
                pieces[base + j] += ref[j].astype(jnp.float32)

        base1 = c * 4 * quarter
        base2 = base1 + rep * 2 * quarter
        base3 = base2 + x * quarter
        stage_c = exchange(0, out1, in1, {"dp": to_c})
        stage_y = exchange(1, out2, in2, {"rep": 1 - rep})
        stage_x = exchange(2, out3, in3, {"dp": to_x})

        def stage_z(step):
            row = lax.rem(z + step, n_z)
            return exchange(
                2 + step, out4.at[row], in4.at[step - 1], {"dp": lax.rem(dp + SPAN * step, n_dp)}
            )

        def rs0():
            text_grads()
            text_grad = image_out[...]
            wide = 16 * tall

            for at in range(0, 8 * n_z, 16):
                product = jnp.dot(
                    feats_turned[pl.ds(at * tall, wide), :], text_grad,
                    preferred_element_type=jnp.float32,
                )
                for i in range(at, at + 16):
                    place = ((i % 4) * 2 + i // 4 % 2) * n_z + i // 8
                    lines = product[(i - at) * tall : (i - at + 1) * tall]
                    pieces[place, pl.ds(0, tall), :] = lines[:, :deep]
                    pieces[place, pl.ds(tall, tall), :] = lines[:, deep:]

            fill(out1, (1 - c) * 4 * quarter)
            stage_c.start()

        def rs1():
            stage_c.wait()
            gain(in1, base1)
            fill(out2, base1 + (1 - rep) * 2 * quarter)
            stage_y.start()

        def rs2():
            stage_y.wait()
            gain(in2, base2)
            fill(out3, base2 + (1 - x) * quarter)
            stage_x.start()

        def rs3():
            stage_x.wait()
            gain(in3, base3)
            fill(out4, base3)
            for step in range(1, n_z):
                stage_z(step).start()

        def rs4():
            total = pieces[base3 + z]
            for step in range(1, n_z):
                stage_z(step).wait()
                total = total + in4[step - 1].astype(jnp.float32)
            proj_out[:, :deep] = total[:tall]
            proj_out[:, deep:] = total[tall:]

    pl.loop(0, 2)(own_tile)

    @pl.loop(0, 4 * CHUNKS)
    def _(s):
        phase = s // CHUNKS
        h = lax.rem(s, CHUNKS)
        kind = phase // 2
        r = 1 + lax.rem(phase, 2)
        arrived(slot_of(kind, r, q), h)

        @pl.when(r == 1)
        def _():
            z_copy(kind, 1, h).start()

        @pl.when(r <= first_of(kind, x) + 1)
        def _():
            x_copy(kind, r, h).start()

        @pl.when(r <= first_of(kind, c) + 1)
        def _():
            c_copy(kind, r, h).start()

        @pl.when(s == 2 * CHUNKS - LEAD)
        def _():
            start_own(1, True, False)

        @pl.when(s >= LAG)
        def _():
            x_step(s - LAG)

        if CHUNKS == 4:
            @pl.when(s >= CHUNKS)
            def _():
                tile_step(s - CHUNKS)

        if summed:
            for at, stage in zip(STAGES, (rs0, rs1, rs2, rs3)):
                @pl.when(s == at)
                def _():
                    stage()

    last = 4 * CHUNKS - LAG

    @pl.loop(0, 4)
    def _(n):
        @pl.when(n < LAG)
        def _():
            x_step(last + n)

        pair_part(12 + 2 * lax.rem(n, 2), n // 2)

        if summed:
            @pl.when(n == 1)
            def _():
                rs3()

    if summed:
        rs4()

    if not summed:
        proj_partial()
        proj_out[...] = partial[...]
    proj_store = pltpu.make_async_copy(proj_out, proj_out_hbm, store.at[0])
    proj_store.start()

    @pl.loop(0, rows // half)
    def _(i):
        part = pl.ds(i * half, half)
        factor = factors[0, part, :]
        normal = images_ref[part, :].astype(jnp.float32) * factor
        upstream = sums[1, part, :]
        image_out[part, :] = (
            factor * (upstream - normal * jnp.sum(normal * upstream, axis=-1, keepdims=True))
        ).astype(jnp.bfloat16)

    image_store = pltpu.make_async_copy(image_out, image_hbm, store.at[1])
    image_store.start()

    @pl.loop(0, 4 * CHUNKS)
    def _(t):
        h = lax.rem(t, CHUNKS)
        i = t // CHUNKS
        kind = i // 2
        e = lax.rem(i, 2)
        z_copy(kind, e, h).wait_send()
        x_copy(kind, first_of(kind, x) + e, h).wait_send()
        c_copy(kind, first_of(kind, c) + e, h).wait_send()
        relay_copy(kind, e, h).wait_send()

    image_store.wait()
    proj_store.wait()


def solution(mesh):
    n_dp, n_rep = mesh.shape["dp"], mesh.shape["rep"]

    def on_device(images, feats, proj, scale, bias):
        rows, width = images.shape
        depth = feats.shape[1]
        share = depth // (n_dp * n_rep)
        n_z = n_dp // SPAN
        summed = n_rep == 2 and share % 8 == 0
        lines = share if summed else depth
        unit = (2 * lines, width // 2) if summed else (16, 128)
        near = n_z if summed else 1
        hbm = pl.BlockSpec(memory_space=pltpu.HBM)
        anywhere = pl.BlockSpec(memory_space=pl.ANY)
        smem = pl.BlockSpec(memory_space=pltpu.SMEM)
        dma = pltpu.SemaphoreType.DMA
        image_grad, proj_grad = pl.pallas_call(
            functools.partial(kernel, n_dp, n_rep, summed),
            out_shape=(
                jax.ShapeDtypeStruct((rows, width), jnp.bfloat16),
                jax.ShapeDtypeStruct((lines, width), jnp.float32),
            ),
            in_specs=[smem, smem, hbm, hbm, hbm],
            out_specs=(anywhere, anywhere),
            scratch_shapes=[
                pltpu.VMEM((6 * SPAN, rows, width), jnp.bfloat16),
                pltpu.VMEM((2, rows, width), jnp.float32),
                pltpu.VMEM((rows, width), jnp.float32),
                pltpu.VMEM((2, rows, 1), jnp.float32),
                pltpu.VMEM((16, 128) if summed else (depth, width), jnp.float32),
                pltpu.VMEM((rows, width), jnp.bfloat16),
                pltpu.VMEM((rows, depth), jnp.bfloat16),
                pltpu.VMEM((depth, width), jnp.bfloat16),
                pltpu.VMEM((rows, width), jnp.bfloat16),
                pltpu.VMEM((lines, width), jnp.float32),
                pltpu.VMEM((depth, rows) if summed else (16, 128), jnp.bfloat16),
                dma((3,)),
                dma((2,)),
                dma((4 * CHUNKS,)),
                dma((4 * CHUNKS,)),
                dma((8 * CHUNKS,)),
                dma((6 * SPAN * CHUNKS,)),
                pltpu.VMEM((8 * near,) + unit, jnp.float32),
                pltpu.VMEM((4 * near,) + unit, jnp.bfloat16),
                pltpu.VMEM((4 * near,) + unit, jnp.bfloat16),
                pltpu.VMEM((2 * near,) + unit, jnp.bfloat16),
                pltpu.VMEM((2 * near,) + unit, jnp.bfloat16),
                pltpu.VMEM((near,) + unit, jnp.bfloat16),
                pltpu.VMEM((near,) + unit, jnp.bfloat16),
                pltpu.VMEM((near,) + unit, jnp.bfloat16),
                pltpu.VMEM((near,) + unit, jnp.bfloat16),
                dma((3 + near,)),
                dma((3 + near,)),
            ],
            compiler_params=pltpu.CompilerParams(
                collective_id=0, has_side_effects=True, vmem_limit_bytes=54400 << 10
            ),
        )(scale, bias, images, feats, proj)
        if not summed:
            proj_grad = lax.psum_scatter(
                proj_grad, ("dp", "rep"), scatter_dimension=0, tiled=True
            )
        return image_grad, proj_grad

    in_specs = (P(("dp", "rep"), None), P(("dp", "rep"), None), P(), P(), P())
    out_specs = (P(("dp", "rep"), None), P(("dp", "rep"), None))
    return jax.shard_map(
        on_device, mesh=mesh, in_specs=in_specs, out_specs=out_specs, check_vma=False
    )
```

```python
import functools

import jax
import jax.numpy as jnp
from jax import lax
from jax.experimental import pallas as pl
from jax.experimental.pallas import tpu as pltpu
from jax.sharding import PartitionSpec as P

MESH = pl.DeviceIdType.MESH
EPS = 1e-06
SHIFTS = 8
SPAN = 4
CHUNKS = 4
LAG = 3
LEAD = 3
STAGES = (11, 12, 14, 17)
FINE = 1
LOG2E = 1.4426950408889634


def kernel(
    n_dp, n_rep, summed,
    scale_ref, bias_ref, images_hbm, feats_hbm, proj_hbm, image_hbm, proj_out_hbm,
    blocks, sums, raw, factors, partial, images_ref, feats_ref, proj_ref, image_out, proj_out,
    feats_turned, load, store, send, recv_z, recv_x, recv_c,
    pieces, out1, in1, out2, in2, out3, in3, out4, in4, rs_send, rs_recv,
):
    rows = images_hbm.shape[0]
    piece = rows // CHUNKS
    half = min(256, rows)
    dp = lax.axis_index("dp")
    rep = lax.axis_index("rep")
    n_z = n_dp // SPAN
    q = lax.rem(dp, SPAN)
    z = dp // SPAN
    x = q // 2
    c = lax.rem(q, 2)
    to_x = dp + 2 - 4 * x
    to_c = dp + 1 - 2 * c
    q_x = q + 2 - 4 * x
    q_c = q + 1 - 2 * c
    q_xc = q_x + 1 - 2 * c
    up = lax.rem(dp + SPAN, n_dp)
    down = lax.rem(dp + n_dp - SPAN, n_dp)

    barrier = pltpu.get_barrier_semaphore()
    greeted = 2
    for target in (to_x, to_c):
        pl.semaphore_signal(barrier, inc=1, device_id={"dp": target}, device_id_type=MESH)
    if summed:
        for step in range(1, n_z):
            pl.semaphore_signal(
                barrier, inc=1, device_id={"dp": lax.rem(dp + SPAN * step, n_dp)}, device_id_type=MESH
            )
        pl.semaphore_signal(barrier, inc=1, device_id={"rep": 1 - rep}, device_id_type=MESH)
        greeted += n_z
    else:
        for target in (up, down):
            pl.semaphore_signal(barrier, inc=1, device_id={"dp": target}, device_id_type=MESH)
        greeted += 2

    loads = [
        pltpu.make_async_copy(source, target, load.at[n])
        for n, (source, target) in enumerate(
            ((images_hbm, images_ref), (proj_hbm, proj_ref), (feats_hbm, feats_ref))
        )
    ]
    for copy in loads:
        copy.start()

    def slot_of(kind, r, place):
        return (kind * 3 + r) * SPAN + place

    def moved(source, target, cut, send, receive, dev):
        return pltpu.make_async_remote_copy(
            src_ref=blocks.at[source, cut, :],
            dst_ref=blocks.at[target, cut, :],
            send_sem=send,
            recv_sem=receive,
            device_id={"dp": dev},
            device_id_type=MESH,
        )

    def coarse(h):
        return pl.ds(pl.multiple_of(h * piece, 16), piece), h

    def cuts(kind, r, h, act):
        if FINE == 1:
            act(*coarse(h))
            return
        fine = (kind == 1) & (r == 2)
        short = piece // FINE

        @pl.loop(0, jnp.where(fine, FINE, 0))
        def _(g):
            mark = h * FINE + g
            act(pl.ds(pl.multiple_of(mark * short, 16), short), mark)

        @pl.when(jnp.logical_not(fine))
        def _():
            act(*coarse(h))

    def half_of(cut):
        return cut.start // (rows // 2)

    def z_copy(kind, r, cut, mark):
        dev = jnp.where(kind == 0, down, up)
        n = kind * 2 + r
        return moved(
            slot_of(kind, r, q), slot_of(kind, r + 1, q), cut,
            send.at[0], recv_z.at[n * CHUNKS + mark], dev,
        )

    def first_of(kind, bit):
        return jnp.where(kind == 0, 1 - bit, bit)

    def x_copy(kind, r, cut, mark):
        s = slot_of(kind, r, q)
        n = kind * 2 + r - first_of(kind, x)
        return moved(s, s, cut, send.at[1], recv_x.at[n * CHUNKS + mark], to_x)

    def c_copy(kind, r, cut, _):
        s = slot_of(kind, r, q)
        n = kind * 2 + r - first_of(kind, c)
        return moved(s, s, cut, send.at[2], recv_c.at[n * 2 + half_of(cut)], to_c)

    def relay_copy(kind, e, cut, _):
        s = slot_of(kind, first_of(kind, 1 - x) + e, q_x)
        n = 4 + kind * 2 + e
        return moved(s, s, cut, send.at[2], recv_c.at[n * 2 + half_of(cut)], to_c)

    def landed(view, semaphore):
        pltpu.make_async_copy(view, view, semaphore).wait()

    def arrived(kind, e, i, s, part):
        view = blocks.at[s, pl.ds(pl.multiple_of(part * (rows // 2), 16), rows // 2), :]
        n = kind * 2 + e + jnp.where(i == 3, 4, 0)
        landed(view, recv_c.at[n * 2 + part])

    def start_own(kind, along=True, across=True):
        first = first_of(kind, x)
        first_c = first_of(kind, c)
        @pl.loop(0, CHUNKS)
        def _(h):
            if along:
                z_copy(kind, 0, *coarse(h)).start()

            @pl.when((first == 0) & across)
            def _():
                x_copy(kind, 0, *coarse(h)).start()

            @pl.when((first_c == 0) & across)
            def _():
                c_copy(kind, 0, *coarse(h)).start()

    scaling = scale_ref[0]
    shifted = bias_ref[0]
    own_u = slot_of(0, 0, q)
    own_v = slot_of(1, 0, q)

    loads[0].wait()

    @pl.loop(0, rows // half)
    def _(i):
        part = pl.ds(i * half, half)
        values = images_ref[part, :].astype(jnp.float32)
        factor = lax.rsqrt(jnp.sum(values * values, axis=-1, keepdims=True) + EPS)
        factors[0, part, :] = factor
        blocks[own_u, part, :] = (values * factor).astype(jnp.bfloat16)

    loads[1].wait()
    loads[2].wait()

    @pl.loop(0, rows // half)
    def _(i):
        part = pl.ds(i * half, half)
        values = jnp.dot(feats_ref[part, :], proj_ref[...], preferred_element_type=jnp.float32)
        factor = lax.rsqrt(jnp.sum(values * values, axis=-1, keepdims=True) + EPS)
        raw[part, :] = values
        factors[1, part, :] = factor
        blocks[own_v, part, :] = (values * factor).astype(jnp.bfloat16)

    if summed:
        feats_turned[...] = feats_ref[...].T

    pl.semaphore_wait(barrier, greeted)
    start_own(0)
    start_own(1, False, True)

    slope = scaling * -LOG2E
    offset = shifted * -LOG2E

    def score(own, part, s, cut):
        return lax.dot_general(
            blocks[own, part, :], blocks[s, cut, :], (((1,), (1,)), ((), ())),
            preferred_element_type=jnp.float32,
        )

    def own_tile(kind):
        own = slot_of(1 - kind, 0, q)
        s = slot_of(kind, 0, q)
        for i in range(rows // half):
            part = pl.ds(i * half, half)
            logits = scaling * score(own, part, s, pl.ds(0, rows)) + shifted
            line = lax.broadcasted_iota(jnp.int32, logits.shape, 0) + i * half
            paired = line == lax.broadcasted_iota(jnp.int32, logits.shape, 1)
            weight = jnp.where(paired, -scaling, scaling) * jax.nn.sigmoid(
                jnp.where(paired, -logits, logits)
            )
            sums[kind, part, :] = jnp.dot(
                weight.astype(jnp.bfloat16), blocks[s], preferred_element_type=jnp.float32
            )

    def tile(kind, cuts):
        own = slot_of(1 - kind, 0, q)
        strips = [pl.ds(i * half, half) for i in range(rows // half)]
        weights = []
        for part in strips:
            for s, cut in cuts:
                grown = 1.0 + jnp.exp2(slope * score(own, part, s, cut) + offset)
                weight = scaling * pltpu.reciprocal(grown, approx=True)
                weights.append(weight.astype(jnp.bfloat16))
        for i, part in enumerate(strips):
            total = sums[kind, part, :]
            for j, (s, cut) in enumerate(cuts):
                total += jnp.dot(
                    weights[i * len(cuts) + j], blocks[s, cut, :],
                    preferred_element_type=jnp.float32,
                )
            sums[kind, part, :] = total

    def x_step(t):
        phase = t // CHUNKS
        h = lax.rem(t, CHUNKS)
        kind = phase // 2
        e = lax.rem(phase, 2)
        r = first_of(kind, 1 - x) + e

        def pass_on(cut, mark):
            landed(blocks.at[slot_of(kind, r, q_x), cut, :], recv_x.at[phase * CHUNKS + mark])
            relay_copy(kind, e, cut, mark).start()

        cuts(kind, r, h, pass_on)

    def block_of(t):
        phase = t // 4
        i = lax.rem(t, 4)
        kind = phase // 2
        e = lax.rem(phase, 2)
        bit = jnp.where(i == 1, 1 - c, 1 - x)
        r = e + jnp.where(i == 0, 1, first_of(kind, bit))
        place = jnp.where(i == 0, q, jnp.where(i == 1, q_c, jnp.where(i == 2, q_x, q_xc)))
        return kind, e, slot_of(kind, r, place), i

    def tile_step(t):
        kind, e, s, i = block_of(t)

        @pl.when(lax.rem(i, 2) == 1)
        def _():
            for part in range(2):
                arrived(kind, e, i, s, part)

        tile(kind, [(s, pl.ds(0, rows))])

    def pair_part(t, part):
        cut = pl.ds(pl.multiple_of(part * (rows // 2), 16), rows // 2)
        kind, _, s, _ = block_of(t)
        _, e, other, i = block_of(t + 1)
        arrived(kind, e, i, other, part)
        tile(kind, [(s, cut), (other, cut)])

    def exchange(stage, source, target, dev):
        return pltpu.make_async_remote_copy(
            src_ref=source, dst_ref=target, send_sem=rs_send.at[stage], recv_sem=rs_recv.at[stage],
            device_id=dev, device_id_type=MESH,
        )

    def text_back(i):
        part = pl.ds(i * half, half)
        factor = factors[1, part, :]
        normal = raw[part, :] * factor
        upstream = sums[0, part, :]
        return factor * (upstream - normal * jnp.sum(normal * upstream, axis=-1, keepdims=True))

    def text_grads():
        @pl.loop(0, rows // half)
        def _(i):
            image_out[pl.ds(i * half, half), :] = text_back(i).astype(jnp.bfloat16)

    def proj_partial():
        text_grads()
        text_grad = image_out[...]
        wide = 256

        @pl.loop(0, feats_ref.shape[1] // wide)
        def _(i):
            cols = pl.ds(pl.multiple_of(i * wide, wide), wide)
            partial[pl.ds(pl.multiple_of(i * wide, wide), wide), :] = lax.dot_general(
                feats_ref[:, cols], text_grad, (((0,), (0,)), ((), ())),
                preferred_element_type=jnp.float32,
            )

    if summed:
        quarter = n_z
        tall = proj_out.shape[0]
        deep = proj_out.shape[1] // 2

        def fill(ref, base):
            @pl.loop(0, ref.shape[0])
            def _(j):
                ref[j] = pieces[base + j].astype(jnp.bfloat16)

        def gain(ref, base):
            @pl.loop(0, ref.shape[0])
            def _(j):
                pieces[base + j] += ref[j].astype(jnp.float32)

        base1 = c * 4 * quarter
        base2 = base1 + rep * 2 * quarter
        base3 = base2 + x * quarter
        stage_c = exchange(0, out1, in1, {"dp": to_c})
        stage_y = exchange(1, out2, in2, {"rep": 1 - rep})
        stage_x = exchange(2, out3, in3, {"dp": to_x})

        def stage_z(step):
            row = lax.rem(z + step, n_z)
            return exchange(
                2 + step, out4.at[row], in4.at[step - 1], {"dp": lax.rem(dp + SPAN * step, n_dp)}
            )

        def rs0():
            text_grads()
            text_grad = image_out[...]
            wide = 16 * tall

            for at in range(0, 8 * n_z, 16):
                product = jnp.dot(
                    feats_turned[pl.ds(at * tall, wide), :], text_grad,
                    preferred_element_type=jnp.float32,
                )
                for i in range(at, at + 16):
                    place = ((i % 4) * 2 + i // 4 % 2) * n_z + i // 8
                    lines = product[(i - at) * tall : (i - at + 1) * tall]
                    pieces[place, pl.ds(0, tall), :] = lines[:, :deep]
                    pieces[place, pl.ds(tall, tall), :] = lines[:, deep:]

            fill(out1, (1 - c) * 4 * quarter)
            stage_c.start()

        def rs1():
            stage_c.wait()
            gain(in1, base1)
            fill(out2, base1 + (1 - rep) * 2 * quarter)
            stage_y.start()

        def rs2():
            stage_y.wait()
            gain(in2, base2)
            fill(out3, base2 + (1 - x) * quarter)
            stage_x.start()

        def rs3():
            stage_x.wait()
            gain(in3, base3)
            fill(out4, base3)
            for step in range(1, n_z):
                stage_z(step).start()

        def rs4():
            total = pieces[base3 + z]
            for step in range(1, n_z):
                stage_z(step).wait()
                total = total + in4[step - 1].astype(jnp.float32)
            proj_out[:, :deep] = total[:tall]
            proj_out[:, deep:] = total[tall:]

    pl.loop(0, 2)(own_tile)

    @pl.loop(0, 4 * CHUNKS)
    def _(s):
        phase = s // CHUNKS
        h = lax.rem(s, CHUNKS)
        kind = phase // 2
        r = 1 + lax.rem(phase, 2)

        def pass_on(cut, mark):
            landed(blocks.at[slot_of(kind, r, q), cut, :], recv_z.at[phase * CHUNKS + mark])

            @pl.when(r == 1)
            def _():
                cuts(kind, 2, h, lambda cut, mark: z_copy(kind, 1, cut, mark).start())

            @pl.when(r <= first_of(kind, x) + 1)
            def _():
                x_copy(kind, r, cut, mark).start()

            @pl.when(r <= first_of(kind, c) + 1)
            def _():
                c_copy(kind, r, cut, mark).start()

        cuts(kind, r, h, pass_on)

        @pl.when(s == 2 * CHUNKS - LEAD)
        def _():
            start_own(1, True, False)

        @pl.when(s >= LAG)
        def _():
            x_step(s - LAG)

        if CHUNKS == 4:
            @pl.when(s >= CHUNKS)
            def _():
                tile_step(s - CHUNKS)

        if summed:
            for at, stage in zip(STAGES, (rs0, rs1, rs2, rs3)):
                @pl.when(s == at)
                def _():
                    stage()

    last = 4 * CHUNKS - LAG

    @pl.loop(0, 4)
    def _(n):
        @pl.when(n < LAG)
        def _():
            x_step(last + n)

        pair_part(12 + 2 * lax.rem(n, 2), n // 2)

        if summed:
            @pl.when(n == 1)
            def _():
                rs3()

    if summed:
        rs4()

    if not summed:
        proj_partial()
        proj_out[...] = partial[...]
    proj_store = pltpu.make_async_copy(proj_out, proj_out_hbm, store.at[0])
    proj_store.start()

    @pl.loop(0, rows // half)
    def _(i):
        part = pl.ds(i * half, half)
        factor = factors[0, part, :]
        normal = images_ref[part, :].astype(jnp.float32) * factor
        upstream = sums[1, part, :]
        image_out[part, :] = (
            factor * (upstream - normal * jnp.sum(normal * upstream, axis=-1, keepdims=True))
        ).astype(jnp.bfloat16)

    image_store = pltpu.make_async_copy(image_out, image_hbm, store.at[1])
    image_store.start()

    for n, count in enumerate((4, 4, 8)):
        landed(blocks.at[pl.ds(0, count)], send.at[n])

    image_store.wait()
    proj_store.wait()


def solution(mesh):
    n_dp, n_rep = mesh.shape["dp"], mesh.shape["rep"]

    def on_device(images, feats, proj, scale, bias):
        rows, width = images.shape
        depth = feats.shape[1]
        share = depth // (n_dp * n_rep)
        n_z = n_dp // SPAN
        summed = n_rep == 2 and share % 8 == 0
        lines = share if summed else depth
        unit = (2 * lines, width // 2) if summed else (16, 128)
        near = n_z if summed else 1
        hbm = pl.BlockSpec(memory_space=pltpu.HBM)
        anywhere = pl.BlockSpec(memory_space=pl.ANY)
        smem = pl.BlockSpec(memory_space=pltpu.SMEM)
        dma = pltpu.SemaphoreType.DMA
        image_grad, proj_grad = pl.pallas_call(
            functools.partial(kernel, n_dp, n_rep, summed),
            out_shape=(
                jax.ShapeDtypeStruct((rows, width), jnp.bfloat16),
                jax.ShapeDtypeStruct((lines, width), jnp.float32),
            ),
            in_specs=[smem, smem, hbm, hbm, hbm],
            out_specs=(anywhere, anywhere),
            scratch_shapes=[
                pltpu.VMEM((6 * SPAN, rows, width), jnp.bfloat16),
                pltpu.VMEM((2, rows, width), jnp.float32),
                pltpu.VMEM((rows, width), jnp.float32),
                pltpu.VMEM((2, rows, 1), jnp.float32),
                pltpu.VMEM((16, 128) if summed else (depth, width), jnp.float32),
                pltpu.VMEM((rows, width), jnp.bfloat16),
                pltpu.VMEM((rows, depth), jnp.bfloat16),
                pltpu.VMEM((depth, width), jnp.bfloat16),
                pltpu.VMEM((rows, width), jnp.bfloat16),
                pltpu.VMEM((lines, width), jnp.float32),
                pltpu.VMEM((depth, rows) if summed else (16, 128), jnp.bfloat16),
                dma((3,)),
                dma((2,)),
                dma((3,)),
                dma(((3 + FINE) * CHUNKS,)),
                dma(((3 + FINE) * CHUNKS,)),
                dma((16,)),
                pltpu.VMEM((8 * near,) + unit, jnp.float32),
                pltpu.VMEM((4 * near,) + unit, jnp.bfloat16),
                pltpu.VMEM((4 * near,) + unit, jnp.bfloat16),
                pltpu.VMEM((2 * near,) + unit, jnp.bfloat16),
                pltpu.VMEM((2 * near,) + unit, jnp.bfloat16),
                pltpu.VMEM((near,) + unit, jnp.bfloat16),
                pltpu.VMEM((near,) + unit, jnp.bfloat16),
                pltpu.VMEM((near,) + unit, jnp.bfloat16),
                pltpu.VMEM((near,) + unit, jnp.bfloat16),
                dma((3 + near,)),
                dma((3 + near,)),
            ],
            compiler_params=pltpu.CompilerParams(
                collective_id=0, has_side_effects=True, vmem_limit_bytes=54400 << 10
            ),
        )(scale, bias, images, feats, proj)
        if not summed:
            proj_grad = lax.psum_scatter(
                proj_grad, ("dp", "rep"), scatter_dimension=0, tiled=True
            )
        return image_grad, proj_grad

    in_specs = (P(("dp", "rep"), None), P(("dp", "rep"), None), P(), P(), P())
    out_specs = (P(("dp", "rep"), None), P(("dp", "rep"), None))
    return jax.shard_map(
        on_device, mesh=mesh, in_specs=in_specs, out_specs=out_specs, check_vma=False
    )
```

```python
import functools

import jax
import jax.numpy as jnp
from jax import lax
from jax.experimental import pallas as pl
from jax.experimental.pallas import tpu as pltpu
from jax.sharding import PartitionSpec as P

MESH = pl.DeviceIdType.MESH
EPS = 1e-06
SHIFTS = 8
SPAN = 4
CHUNKS = 4
LAG = 3
LEAD = 3
STAGES = (11, 12, 14, 17)
FINE = 1
LOG2E = 1.4426950408889634


def kernel(
    n_dp, n_rep, summed,
    scale_ref, bias_ref, images_hbm, feats_hbm, proj_hbm, image_out, proj_out,
    blocks, sums, raw, factors, partial, images_ref, feats_ref, proj_ref,
    feats_turned, load, send, recv_z, recv_x, recv_c,
    pieces, out1, in1, out2, in2, out3, in3, out4, in4, rs_send, rs_recv,
):
    rows = images_hbm.shape[0]
    piece = rows // CHUNKS
    half = min(256, rows)
    dp = lax.axis_index("dp")
    rep = lax.axis_index("rep")
    n_z = n_dp // SPAN
    q = lax.rem(dp, SPAN)
    z = dp // SPAN
    x = q // 2
    c = lax.rem(q, 2)
    to_x = dp + 2 - 4 * x
    to_c = dp + 1 - 2 * c
    q_x = q + 2 - 4 * x
    q_c = q + 1 - 2 * c
    q_xc = q_x + 1 - 2 * c
    up = lax.rem(dp + SPAN, n_dp)
    down = lax.rem(dp + n_dp - SPAN, n_dp)

    barrier = pltpu.get_barrier_semaphore()
    greeted = 2
    if summed:
        for step in range(1, n_z):
            pl.semaphore_signal(
                barrier, inc=1, device_id={"dp": lax.rem(dp + SPAN * step, n_dp)}, device_id_type=MESH
            )
        pl.semaphore_signal(barrier, inc=1, device_id={"rep": 1 - rep}, device_id_type=MESH)
        greeted += n_z
    else:
        for target in (up, down):
            pl.semaphore_signal(barrier, inc=1, device_id={"dp": target}, device_id_type=MESH)
        greeted += 2

    for target in (to_x, to_c):
        pl.semaphore_signal(barrier, inc=1, device_id={"dp": target}, device_id_type=MESH)

    loads = [
        pltpu.make_async_copy(source, target, load.at[n])
        for n, (source, target) in enumerate(
            ((images_hbm, images_ref), (proj_hbm, proj_ref), (feats_hbm, feats_ref))
        )
    ]
    for copy in loads:
        copy.start()

    def slot_of(kind, r, place):
        return (kind * 3 + r) * SPAN + place

    def moved(source, target, cut, send, receive, dev):
        return pltpu.make_async_remote_copy(
            src_ref=blocks.at[source, cut, :],
            dst_ref=blocks.at[target, cut, :],
            send_sem=send,
            recv_sem=receive,
            device_id={"dp": dev},
            device_id_type=MESH,
        )

    def coarse(h):
        return pl.ds(pl.multiple_of(h * piece, 16), piece), h

    def cuts(kind, r, h, act):
        if FINE == 1:
            act(*coarse(h))
            return
        fine = (kind == 1) & (r == 2)
        short = piece // FINE

        @pl.loop(0, jnp.where(fine, FINE, 0))
        def _(g):
            mark = h * FINE + g
            act(pl.ds(pl.multiple_of(mark * short, 16), short), mark)

        @pl.when(jnp.logical_not(fine))
        def _():
            act(*coarse(h))

    def half_of(cut):
        return cut.start // (rows // 2)

    def z_copy(kind, r, cut, mark):
        dev = jnp.where(kind == 0, down, up)
        n = kind * 2 + r
        return moved(
            slot_of(kind, r, q), slot_of(kind, r + 1, q), cut,
            send.at[0], recv_z.at[n * CHUNKS + mark], dev,
        )

    def first_of(kind, bit):
        return jnp.where(kind == 0, 1 - bit, bit)

    def x_copy(kind, r, cut, mark):
        s = slot_of(kind, r, q)
        n = kind * 2 + r - first_of(kind, x)
        return moved(s, s, cut, send.at[1], recv_x.at[n * CHUNKS + mark], to_x)

    def c_copy(kind, r, cut, _):
        s = slot_of(kind, r, q)
        n = kind * 2 + r - first_of(kind, c)
        return moved(s, s, cut, send.at[2], recv_c.at[n * 2 + half_of(cut)], to_c)

    def relay_copy(kind, e, cut, _):
        s = slot_of(kind, first_of(kind, 1 - x) + e, q_x)
        n = 4 + kind * 2 + e
        return moved(s, s, cut, send.at[2], recv_c.at[n * 2 + half_of(cut)], to_c)

    def landed(view, semaphore):
        pltpu.make_async_copy(view, view, semaphore).wait()

    def arrived(kind, e, i, s, part):
        view = blocks.at[s, pl.ds(pl.multiple_of(part * (rows // 2), 16), rows // 2), :]
        n = kind * 2 + e + jnp.where(i == 3, 4, 0)
        landed(view, recv_c.at[n * 2 + part])

    def start_own(kind, along=True, across=True):
        first = first_of(kind, x)
        first_c = first_of(kind, c)
        @pl.loop(0, CHUNKS)
        def _(h):
            if along:
                z_copy(kind, 0, *coarse(h)).start()

            @pl.when((first == 0) & across)
            def _():
                x_copy(kind, 0, *coarse(h)).start()

            @pl.when((first_c == 0) & across)
            def _():
                c_copy(kind, 0, *coarse(h)).start()

    scaling = scale_ref[0]
    shifted = bias_ref[0]
    own_u = slot_of(0, 0, q)
    own_v = slot_of(1, 0, q)

    loads[0].wait()

    @pl.loop(0, rows // half)
    def _(i):
        part = pl.ds(i * half, half)
        values = images_ref[part, :].astype(jnp.float32)
        factor = lax.rsqrt(jnp.sum(values * values, axis=-1, keepdims=True) + EPS)
        factors[0, part, :] = factor
        blocks[own_u, part, :] = (values * factor).astype(jnp.bfloat16)

    loads[1].wait()
    loads[2].wait()

    @pl.loop(0, rows // half)
    def _(i):
        part = pl.ds(i * half, half)
        values = jnp.dot(feats_ref[part, :], proj_ref[...], preferred_element_type=jnp.float32)
        factor = lax.rsqrt(jnp.sum(values * values, axis=-1, keepdims=True) + EPS)
        raw[part, :] = values
        factors[1, part, :] = factor
        blocks[own_v, part, :] = (values * factor).astype(jnp.bfloat16)

    if summed:
        feats_turned[...] = feats_ref[...].T

    pl.semaphore_wait(barrier, greeted)
    @pl.when(x == 1)
    def _():
        z_copy(1, 0, *coarse(0)).start()

    start_own(0)
    start_own(1, False, True)

    slope = scaling * -LOG2E
    offset = shifted * -LOG2E

    def score(own, part, s, cut):
        return lax.dot_general(
            blocks[own, part, :], blocks[s, cut, :], (((1,), (1,)), ((), ())),
            preferred_element_type=jnp.float32,
        )

    def own_tile(kind):
        own = slot_of(1 - kind, 0, q)
        s = slot_of(kind, 0, q)
        for i in range(rows // half):
            part = pl.ds(i * half, half)
            logits = scaling * score(own, part, s, pl.ds(0, rows)) + shifted
            line = lax.broadcasted_iota(jnp.int32, logits.shape, 0) + i * half
            paired = line == lax.broadcasted_iota(jnp.int32, logits.shape, 1)
            weight = jnp.where(paired, -scaling, scaling) * jax.nn.sigmoid(
                jnp.where(paired, -logits, logits)
            )
            sums[kind, part, :] = jnp.dot(
                weight.astype(jnp.bfloat16), blocks[s], preferred_element_type=jnp.float32
            )

    def tile(kind, cuts):
        own = slot_of(1 - kind, 0, q)
        strips = [pl.ds(i * half, half) for i in range(rows // half)]
        weights = []
        for part in strips:
            for s, cut in cuts:
                grown = 1.0 + jnp.exp2(slope * score(own, part, s, cut) + offset)
                weight = scaling * pltpu.reciprocal(grown, approx=True)
                weights.append(weight.astype(jnp.bfloat16))
        for i, part in enumerate(strips):
            total = sums[kind, part, :]
            for j, (s, cut) in enumerate(cuts):
                total += jnp.dot(
                    weights[i * len(cuts) + j], blocks[s, cut, :],
                    preferred_element_type=jnp.float32,
                )
            sums[kind, part, :] = total

    def x_step(t):
        phase = t // CHUNKS
        h = lax.rem(t, CHUNKS)
        kind = phase // 2
        e = lax.rem(phase, 2)
        r = first_of(kind, 1 - x) + e

        def pass_on(cut, mark):
            landed(blocks.at[slot_of(kind, r, q_x), cut, :], recv_x.at[phase * CHUNKS + mark])
            relay_copy(kind, e, cut, mark).start()

        cuts(kind, r, h, pass_on)

    def block_of(t):
        phase = t // 4
        i = lax.rem(t, 4)
        kind = phase // 2
        e = lax.rem(phase, 2)
        bit = jnp.where(i == 1, 1 - c, 1 - x)
        r = e + jnp.where(i == 0, 1, first_of(kind, bit))
        place = jnp.where(i == 0, q, jnp.where(i == 1, q_c, jnp.where(i == 2, q_x, q_xc)))
        return kind, e, slot_of(kind, r, place), i

    def tile_step(t):
        kind, e, s, i = block_of(t)

        @pl.when(lax.rem(i, 2) == 1)
        def _():
            for part in range(2):
                arrived(kind, e, i, s, part)

        tile(kind, [(s, pl.ds(0, rows))])

    def pair_part(t, part):
        cut = pl.ds(pl.multiple_of(part * (rows // 2), 16), rows // 2)
        kind, _, s, _ = block_of(t)
        _, e, other, i = block_of(t + 1)
        arrived(kind, e, i, other, part)
        tile(kind, [(s, cut), (other, cut)])

    def exchange(stage, source, target, dev):
        return pltpu.make_async_remote_copy(
            src_ref=source, dst_ref=target, send_sem=rs_send.at[stage], recv_sem=rs_recv.at[stage],
            device_id=dev, device_id_type=MESH,
        )

    def text_back(i):
        part = pl.ds(i * half, half)
        factor = factors[1, part, :]
        normal = raw[part, :] * factor
        upstream = sums[0, part, :]
        return factor * (upstream - normal * jnp.sum(normal * upstream, axis=-1, keepdims=True))

    def text_grads():
        @pl.loop(0, rows // half)
        def _(i):
            image_out[pl.ds(i * half, half), :] = text_back(i).astype(jnp.bfloat16)

    def proj_partial():
        text_grads()
        text_grad = image_out[...]
        wide = 256

        @pl.loop(0, feats_ref.shape[1] // wide)
        def _(i):
            cols = pl.ds(pl.multiple_of(i * wide, wide), wide)
            partial[pl.ds(pl.multiple_of(i * wide, wide), wide), :] = lax.dot_general(
                feats_ref[:, cols], text_grad, (((0,), (0,)), ((), ())),
                preferred_element_type=jnp.float32,
            )

    if summed:
        quarter = n_z
        tall = proj_out.shape[0]
        deep = proj_out.shape[1] // 2

        def fill(ref, base):
            @pl.loop(0, ref.shape[0])
            def _(j):
                ref[j] = pieces[base + j].astype(jnp.bfloat16)

        def gain(ref, base):
            @pl.loop(0, ref.shape[0])
            def _(j):
                pieces[base + j] += ref[j].astype(jnp.float32)

        base1 = c * 4 * quarter
        base2 = base1 + rep * 2 * quarter
        base3 = base2 + x * quarter
        stage_c = exchange(0, out1, in1, {"dp": to_c})
        stage_y = exchange(1, out2, in2, {"rep": 1 - rep})
        stage_x = exchange(2, out3, in3, {"dp": to_x})

        def stage_z(step):
            row = lax.rem(z + step, n_z)
            return exchange(
                2 + step, out4.at[row], in4.at[step - 1], {"dp": lax.rem(dp + SPAN * step, n_dp)}
            )

        def rs0():
            text_grads()
            text_grad = image_out[...]
            wide = 16 * tall

            for at in range(0, 8 * n_z, 16):
                product = jnp.dot(
                    feats_turned[pl.ds(at * tall, wide), :], text_grad,
                    preferred_element_type=jnp.float32,
                )
                for i in range(at, at + 16):
                    place = ((i % 4) * 2 + i // 4 % 2) * n_z + i // 8
                    lines = product[(i - at) * tall : (i - at + 1) * tall]
                    pieces[place, pl.ds(0, tall), :] = lines[:, :deep]
                    pieces[place, pl.ds(tall, tall), :] = lines[:, deep:]

            fill(out1, (1 - c) * 4 * quarter)
            stage_c.start()

        def rs1():
            stage_c.wait()
            gain(in1, base1)
            fill(out2, base1 + (1 - rep) * 2 * quarter)
            stage_y.start()

        def rs2():
            stage_y.wait()
            gain(in2, base2)
            fill(out3, base2 + (1 - x) * quarter)
            stage_x.start()

        def rs3():
            stage_x.wait()
            gain(in3, base3)
            fill(out4, base3)
            for step in range(1, n_z):
                stage_z(step).start()

        def rs4():
            total = pieces[base3 + z]
            for step in range(1, n_z):
                stage_z(step).wait()
                total = total + in4[step - 1].astype(jnp.float32)
            proj_out[:, :deep] = total[:tall]
            proj_out[:, deep:] = total[tall:]

    pl.loop(0, 2)(own_tile)

    @pl.loop(0, 4 * CHUNKS)
    def _(s):
        phase = s // CHUNKS
        h = lax.rem(s, CHUNKS)
        kind = phase // 2
        r = 1 + lax.rem(phase, 2)

        def pass_on(cut, mark):
            landed(blocks.at[slot_of(kind, r, q), cut, :], recv_z.at[phase * CHUNKS + mark])

            @pl.when(r == 1)
            def _():
                cuts(kind, 2, h, lambda cut, mark: z_copy(kind, 1, cut, mark).start())

            @pl.when(r <= first_of(kind, x) + 1)
            def _():
                x_copy(kind, r, cut, mark).start()

            @pl.when(r <= first_of(kind, c) + 1)
            def _():
                c_copy(kind, r, cut, mark).start()

        cuts(kind, r, h, pass_on)

        @pl.when(s == 2 * CHUNKS - LEAD)
        def _():
            @pl.loop(x, CHUNKS)
            def _(h):
                z_copy(1, 0, *coarse(h)).start()

        @pl.when(s >= LAG)
        def _():
            x_step(s - LAG)

        if CHUNKS == 4:
            @pl.when(s >= CHUNKS)
            def _():
                tile_step(s - CHUNKS)

        if summed:
            for at, stage in zip(STAGES, (rs0, rs1, rs2, rs3)):
                @pl.when(s == at)
                def _():
                    stage()

    last = 4 * CHUNKS - LAG

    @pl.loop(0, 4)
    def _(n):
        @pl.when(n < LAG)
        def _():
            x_step(last + n)

        pair_part(12 + 2 * lax.rem(n, 2), n // 2)

        if summed:
            @pl.when(n == 1)
            def _():
                rs3()

    if summed:
        rs4()

    if not summed:
        proj_partial()
        proj_out[...] = partial[...]

    @pl.loop(0, rows // half)
    def _(i):
        part = pl.ds(i * half, half)
        factor = factors[0, part, :]
        normal = images_ref[part, :].astype(jnp.float32) * factor
        upstream = sums[1, part, :]
        image_out[part, :] = (
            factor * (upstream - normal * jnp.sum(normal * upstream, axis=-1, keepdims=True))
        ).astype(jnp.bfloat16)

    for n, count in enumerate((4, 4, 8)):
        landed(blocks.at[pl.ds(0, count)], send.at[n])


def solution(mesh):
    n_dp, n_rep = mesh.shape["dp"], mesh.shape["rep"]

    def on_device(images, feats, proj, scale, bias):
        rows, width = images.shape
        depth = feats.shape[1]
        share = depth // (n_dp * n_rep)
        n_z = n_dp // SPAN
        summed = n_rep == 2 and share % 8 == 0
        lines = share if summed else depth
        unit = (2 * lines, width // 2) if summed else (16, 128)
        near = n_z if summed else 1
        hbm = pl.BlockSpec(memory_space=pltpu.HBM)
        vmem = pl.BlockSpec(memory_space=pltpu.VMEM)
        smem = pl.BlockSpec(memory_space=pltpu.SMEM)
        dma = pltpu.SemaphoreType.DMA
        image_grad, proj_grad = pl.pallas_call(
            functools.partial(kernel, n_dp, n_rep, summed),
            out_shape=(
                jax.ShapeDtypeStruct((rows, width), jnp.bfloat16),
                jax.ShapeDtypeStruct((lines, width), jnp.float32),
            ),
            in_specs=[smem, smem, hbm, hbm, hbm],
            out_specs=(vmem, vmem),
            scratch_shapes=[
                pltpu.VMEM((6 * SPAN, rows, width), jnp.bfloat16),
                pltpu.VMEM((2, rows, width), jnp.float32),
                pltpu.VMEM((rows, width), jnp.float32),
                pltpu.VMEM((2, rows, 1), jnp.float32),
                pltpu.VMEM((16, 128) if summed else (depth, width), jnp.float32),
                pltpu.VMEM((rows, width), jnp.bfloat16),
                pltpu.VMEM((rows, depth), jnp.bfloat16),
                pltpu.VMEM((depth, width), jnp.bfloat16),
                pltpu.VMEM((depth, rows) if summed else (16, 128), jnp.bfloat16),
                dma((3,)),
                dma((3,)),
                dma(((3 + FINE) * CHUNKS,)),
                dma(((3 + FINE) * CHUNKS,)),
                dma((16,)),
                pltpu.VMEM((8 * near,) + unit, jnp.float32),
                pltpu.VMEM((4 * near,) + unit, jnp.bfloat16),
                pltpu.VMEM((4 * near,) + unit, jnp.bfloat16),
                pltpu.VMEM((2 * near,) + unit, jnp.bfloat16),
                pltpu.VMEM((2 * near,) + unit, jnp.bfloat16),
                pltpu.VMEM((near,) + unit, jnp.bfloat16),
                pltpu.VMEM((near,) + unit, jnp.bfloat16),
                pltpu.VMEM((near,) + unit, jnp.bfloat16),
                pltpu.VMEM((near,) + unit, jnp.bfloat16),
                dma((3 + near,)),
                dma((3 + near,)),
            ],
            compiler_params=pltpu.CompilerParams(
                collective_id=0, has_side_effects=True, vmem_limit_bytes=54400 << 10
            ),
        )(scale, bias, images, feats, proj)
        if not summed:
            proj_grad = lax.psum_scatter(
                proj_grad, ("dp", "rep"), scatter_dimension=0, tiled=True
            )
        return image_grad, proj_grad

    in_specs = (P(("dp", "rep"), None), P(("dp", "rep"), None), P(), P(), P())
    out_specs = (P(("dp", "rep"), None), P(("dp", "rep"), None))
    return jax.shard_map(
        on_device, mesh=mesh, in_specs=in_specs, out_specs=out_specs, check_vma=False
    )
```
